1024 devices in a mesh: segment: 8 (over z), frame: 32 (over x_hi, y), row: 4 (over x_lo, core).
Axes of the slice: x: 8 (x_hi: 4, x_lo: 2; x = x_hi * 2 + x_lo), y: 8, z: 8, core: 2. Of those that a mesh axis runs over, the one named last changes fastest.
Arguments:
- clip_tokens: bfloat16 [8, 32, 4, 2, 64, 1536], P('segment', 'frame', 'row'), may hold values from -6 to 6
- qkv_weight: bfloat16 [8, 1536, 2304], P('segment'), may hold values from -1 to 1
- out_weight: bfloat16 [8, 768, 1536], P('segment'), may hold values from -0.21875 to 0.21875
- modulation: bfloat16 [8, 8, 3, 1536], P('segment'), may hold values from -4 to 4
- domain_ids: int32 [8], P('segment'), may hold values from 0 to 7
- tile_lists: int32 [32, 4, 2, 6], P('frame', 'row'), may hold values from 0 to 9, as said below
Outputs:
- handed: bfloat16 [8, 32, 4, 2, 64, 1536], P('segment', 'frame', 'row')
The draws below stay inside these ranges and needn't reach their ends.
Inputs may be any that keep to these rules, and one draw needn't show every extreme that they name: `tile_lists`: each row names 6 different candidates, always the tile's own one, and never a tile outside the grid.
All inputs are finite; a program needn't handle non-finite values.
Results may differ from the reference program's by a relative error of at most 0.0081.
Values may be sent and summed in bfloat16 or wider, within the bound.
A program may use at most 32 MiB of HBM per device.

```python
from functools import partial
import jax
import jax.numpy as jnp
from jax import lax

D = 1536
HEADS = 6
HD = 128
DOMAINS = 8
TILE = 64
COL_TILES = 2
K_ATT = 6
CLIPS = 8
FT = 32
RT = 4


def draw_clip_tokens(key, part):
    full_shape = (CLIPS, FT, RT, COL_TILES, TILE, D)
    sample = jax.random.normal(key, full_shape, jnp.float32)
    return jnp.clip(sample, -6.0, 6.0).astype(jnp.bfloat16)


def draw_qkv_weight(key, part):
    inner_width = HEADS * HD
    sample = jnp.clip(jax.random.normal(key, (CLIPS, D, 3 * inner_width), jnp.float32), -6.0, 6.0) * D ** (-0.5)
    return jnp.clip(sample, -1.0, 1.0).astype(jnp.bfloat16)


def draw_domain_ids(key, part):
    order = jax.random.permutation(jax.random.fold_in(key, 31), CLIPS).astype(jnp.int32)
    offset = jax.random.randint(jax.random.fold_in(key, 37), (CLIPS,), 0, DOMAINS * 4099, dtype=jnp.int32)
    return ((order + offset) % DOMAINS).astype(jnp.int32)


def draw_tile_lists(key, part):
    cand_count = 5 * COL_TILES
    numbers = jnp.arange(cand_count, dtype=jnp.int32)
    slot_of = numbers // COL_TILES
    column_of = numbers % COL_TILES
    frame_pos = jnp.arange(FT, dtype=jnp.int32)[:, None, None, None]
    row_pos = jnp.arange(RT, dtype=jnp.int32)[None, :, None, None]
    own_col = jnp.arange(COL_TILES, dtype=jnp.int32)[None, None, :, None]
    usable = jnp.ones((FT, RT, COL_TILES, cand_count), dtype=bool)
    usable = usable & ~((slot_of == 1) & (frame_pos == 0))
    usable = usable & ~((slot_of == 2) & (frame_pos == FT - 1))
    usable = usable & ~((slot_of == 3) & (row_pos == 0))
    usable = usable & ~((slot_of == 4) & (row_pos == RT - 1))
    itself = (slot_of == 0) & (column_of == own_col)
    ranking = jax.random.randint(key, (FT, RT, COL_TILES, cand_count), 0, 1 << 20, dtype=jnp.int32) * cand_count + numbers
    top_mark = jnp.int32((1 << 20) * cand_count + cand_count)
    marked = jnp.where(itself, top_mark, jnp.where(usable, ranking, -1 - numbers))
    marked = jnp.broadcast_to(marked, (FT, RT, COL_TILES, cand_count))
    _, chosen = lax.top_k(marked, K_ATT)
    return chosen.astype(jnp.int32)


def block_levels(stream_key, extent, split, low, largest):
    def one(dim, shards_of):
        heights = jax.random.uniform(jax.random.fold_in(jax.random.fold_in(stream_key, 6), dim), (shards_of,), jnp.float32, low / len(split), largest / len(split))
        return jnp.repeat(jnp.exp(heights), extent[dim] // shards_of).reshape((-1,) + (1,) * (len(extent) - dim - 1))

    gain = one(*split[0])
    for cut in split[1:]:
        gain = gain * one(*cut)
    return gain


def noise(own_key, dims, width, most, cuts=(), held_as=jnp.bfloat16):
    result = width * jax.random.normal(own_key, dims, jnp.float32)
    if cuts:
        result = result * block_levels(own_key, dims, cuts, -0.22, 0.18)
    return jnp.clip(result, -most, most).astype(held_as)


def setup_inputs(seed: int = 0) -> dict:
    streams_of = jax.random.split(jax.random.key(seed), 7)
    clip_tokens = draw_clip_tokens(jax.random.fold_in(streams_of[6], 71), 0)
    qkv_weight = draw_qkv_weight(jax.random.fold_in(streams_of[6], 71), 0)
    out_weight = noise(streams_of[2], (CLIPS, HEADS * HD, D), (HEADS * HD) ** -0.5, 0.21875, ((0, 8),))
    modulation = noise(streams_of[3], (CLIPS, DOMAINS, 3, D), 1.0, 4.0, ((0, 8),))
    domain_ids = draw_domain_ids(jax.random.fold_in(streams_of[6], 71), 0)
    tile_lists = draw_tile_lists(jax.random.fold_in(streams_of[6], 71), 0)
    return dict(clip_tokens=clip_tokens, qkv_weight=qkv_weight, out_weight=out_weight, modulation=modulation, domain_ids=domain_ids, tile_lists=tile_lists)


epsilon = 1e-06

def normalize(rows, modulate):
    values = rows.astype(jnp.float32)
    row_mean = lax.optimization_barrier(jnp.mean(values, axis=-1, keepdims=True))
    centered = values - row_mean
    row_var = lax.optimization_barrier(jnp.mean(centered * centered, axis=-1, keepdims=True))
    scaled = centered * lax.rsqrt(row_var + epsilon)
    return (scaled * (1.0 + modulate[1]) + modulate[0]).astype(jnp.bfloat16)

def pick_row(cand_row, chosen_row):
    return cand_row[chosen_row]

def attend_frame(operands):
    queries, candidates, chosen = operands
    picked = jax.vmap(pick_row)(candidates, chosen)
    rows_t, col_t, count_k, tile_len, double_width = picked.shape
    inner_width = double_width // 2
    key_count = count_k * tile_len
    picked = picked.reshape(rows_t, col_t, key_count, double_width)
    key_rows = picked[..., :inner_width].reshape(rows_t, col_t, key_count, HEADS, HD).astype(jnp.float32)
    value_rows = picked[..., inner_width:].reshape(rows_t, col_t, key_count, HEADS, HD).astype(jnp.float32)
    query_rows = queries.reshape(rows_t, col_t, tile_len, HEADS, HD).astype(jnp.float32)
    scores = jnp.einsum('rtqhd,rtkhd->rthqk', query_rows, key_rows) * HD ** (-0.5)
    row_peak = lax.optimization_barrier(jnp.max(scores, axis=-1, keepdims=True))
    raised = jnp.exp(scores - row_peak)
    attn_weights = (raised / lax.optimization_barrier(jnp.sum(raised, axis=-1, keepdims=True))).astype(jnp.bfloat16)
    mixed_heads = jnp.einsum('rthqk,rtkhd->rtqhd', attn_weights.astype(jnp.float32), value_rows)
    return mixed_heads.astype(jnp.bfloat16).reshape(rows_t, col_t, tile_len, inner_width)

def one_clip(tile_lists, operands):
    tokens, qkv_part, out_part, modulation_part, domain_part = operands
    frames_t, rows_t, col_t, tile_len, model_width = tokens.shape
    inner_width = HEADS * HD
    modulate = modulation_part[domain_part].astype(jnp.float32)
    own_rows = tokens.reshape(-1, model_width)
    normed = normalize(own_rows, modulate)
    projected = jnp.dot(normed, qkv_part, preferred_element_type=jnp.float32)
    queries = projected[:, :inner_width].astype(jnp.bfloat16).reshape(frames_t, rows_t, col_t, tile_len, inner_width)
    pairs = projected[:, inner_width:].astype(jnp.bfloat16).reshape(frames_t, rows_t, col_t, tile_len, 2 * inner_width)
    padded = jnp.pad(pairs, ((1, 1), (1, 1), (0, 0), (0, 0), (0, 0)))
    candidates = jnp.concatenate([padded[1:-1, 1:-1], padded[:-2, 1:-1], padded[2:, 1:-1], padded[1:-1, :-2], padded[1:-1, 2:]], axis=2)
    mixed = lax.map(attend_frame, (queries, candidates, tile_lists))
    branch = jnp.dot(mixed.reshape(-1, inner_width), out_part, preferred_element_type=jnp.float32)
    finished = own_rows.astype(jnp.float32) + modulate[2] * branch
    return finished.astype(jnp.bfloat16).reshape(tokens.shape)

def reference(clip_tokens, qkv_weight, out_weight, modulation, domain_ids, tile_lists):
    finished = lax.map(partial(one_clip, tile_lists), (clip_tokens, qkv_weight, out_weight, modulation, domain_ids))
    return jnp.roll(finished, 1, axis=0)
```

```python
import functools

import jax
import jax.numpy as jnp
from jax import lax
from jax.experimental import pallas as pl
from jax.experimental.pallas import tpu as pltpu
from jax.sharding import PartitionSpec as P

MESH = pl.DeviceIdType.MESH
HD = 128
HEADS = 6
INNER = HEADS * HD
D = 1536
ROWS = 128
TILE = 64
SLOTS = 5
KEYS = SLOTS * ROWS
NREL = 3
EPS = 1e-06
MASKED = -1e30


def kernel(
    n_frame, n_row, n_seg, group,
    dom_ref, x_hbm, w_hbm, wo_hbm, mod_hbm, lists_hbm,
    out_ref,
    x_v, normed, wkv, wq, wo, mod_v, lists_v,
    kv, relay, qs, bias, mixed, acc, fin,
    in_sem, wkv_sem, send_sem, recv_sem, rsend_sem, rrecv_sem, hand_send, hand_recv,
):
    f = lax.axis_index("frame")
    r = lax.axis_index("row")
    s = lax.axis_index("segment")
    y = lax.rem(f, group)
    g = lax.div(f, group)
    last_g = n_frame // group - 1

    small = [
        pltpu.make_async_copy(x_hbm, x_v, in_sem.at[0]),
        pltpu.make_async_copy(mod_hbm, mod_v, in_sem.at[1]),
        pltpu.make_async_copy(lists_hbm, lists_v, in_sem.at[3]),
    ]
    for c in small:
        c.start()
    kv_in = []
    for h in range(HEADS):
        pair = []
        for part in range(2):
            c = pltpu.make_async_copy(
                w_hbm.at[:, pl.ds(INNER * (1 + part) + HD * h, HD)],
                wkv.at[h, :, pl.ds(HD * part, HD)],
                wkv_sem.at[h, part],
            )
            c.start()
            pair.append(c)
        kv_in.append(pair)
    q_in = pltpu.make_async_copy(w_hbm.at[:, pl.ds(0, INNER)], wq, in_sem.at[4])
    q_in.start()
    wo_in = pltpu.make_async_copy(wo_hbm, wo, in_sem.at[5])
    wo_in.start()

    has_next = f < n_frame - 1
    has_prev = f > 0
    has_up = r < n_row - 1
    has_dn = r > 0
    edge_next = (y == group - 1) & (g < last_g)
    edge_prev = (y == 0) & (g > 0)
    relay_next = (y == 0) & (g < last_g)
    relay_prev = (y == group - 1) & (g > 0)

    barrier = pltpu.get_barrier_semaphore()
    peers = [
        (has_next, {"frame": f + 1}),
        (has_prev, {"frame": f - 1}),
        (has_up, {"row": r + 1}),
        (has_dn, {"row": r - 1}),
        (edge_next, {"frame": f - (group - 1)}),
        (edge_next, {"frame": f + group}),
        (edge_prev, {"frame": f + (group - 1)}),
        (edge_prev, {"frame": f - group}),
        (relay_next, {"frame": f + (group - 1)}),
        (relay_next, {"frame": f + group}),
        (relay_prev, {"frame": f - (group - 1)}),
        (relay_prev, {"frame": f - group}),
        (None, {"segment": lax.rem(s + n_seg - 1, n_seg)}),
    ]
    def when(cond):
        return (lambda act: act()) if cond is None else pl.when(cond)

    for cond, dev in peers:
        @when(cond)
        def _(dev=dev):
            pl.semaphore_signal(barrier, inc=1, device_id=dev, device_id_type=MESH)

    for cond, slot in ((f == 0, 1), (f == n_frame - 1, 2), (r == 0, 3), (r == n_row - 1, 4)):
        @pl.when(cond)
        def _(slot=slot):
            kv[slot] = jnp.zeros((HEADS, ROWS, 2 * HD), jnp.bfloat16)

    for c in small:
        c.wait()

    domains = mod_v.shape[1]
    mine = lax.broadcasted_iota(jnp.int32, (domains, D), 0) == dom_ref[0]

    def of_domain(i):
        return jnp.sum(jnp.where(mine, mod_v[i].astype(jnp.float32), 0.0), axis=0, keepdims=True)

    shift = of_domain(0)
    scale = 1.0 + of_domain(1)
    gate = of_domain(2)

    def norm_rows(i, _):
        rows = pl.ds(pl.multiple_of(i * 16, 16), 16)
        values = x_v[rows, :].astype(jnp.float32)
        mean = jnp.sum(values, axis=-1, keepdims=True) * (1.0 / D)
        centered = values - mean
        var = jnp.sum(centered * centered, axis=-1, keepdims=True) * (1.0 / D)
        normed[rows, :] = (centered * lax.rsqrt(var + EPS) * scale + shift).astype(jnp.bfloat16)
        return 0

    lax.fori_loop(0, ROWS // 16, norm_rows, 0, unroll=2)

    lists = lists_v[...]
    cand = lax.broadcasted_iota(jnp.int32, (2, KEYS), 1) // TILE
    hit = jnp.zeros((2, KEYS), jnp.float32)
    for j in range(lists.shape[1]):
        hit = jnp.where(cand == lists[:, j : j + 1], 1.0, hit)
    open_keys = jnp.where(hit > 0.5, 0.0, MASKED)
    for t in range(2):
        bias[pl.ds(t * TILE, TILE), :] = jnp.broadcast_to(open_keys[t : t + 1], (TILE, KEYS))

    greeted = 1
    for cond, _ in peers[:-1]:
        greeted += cond.astype(jnp.int32)
    pl.semaphore_wait(barrier, greeted)

    def copy_to(src, dst, send, recv, dev):
        return pltpu.make_async_remote_copy(
            src_ref=src, dst_ref=dst, send_sem=send, recv_sem=recv,
            device_id=dev, device_id_type=MESH,
        )

    def direct(slot, h, dev):
        return copy_to(kv.at[0, h], kv.at[slot, h], send_sem.at[slot - 1, h], recv_sem.at[slot - 1, h], dev)

    def to_relay(slot, h, dev):
        return copy_to(kv.at[0, h], relay.at[h], send_sem.at[slot - 1, h], rrecv_sem.at[h], dev)

    def onward(slot, h, dev):
        return copy_to(relay.at[h], kv.at[slot, h], rsend_sem.at[h], recv_sem.at[slot - 1, h], dev)

    for h in range(HEADS):
        for c in kv_in[h]:
            c.wait()
        kv[0, h] = jnp.dot(
            normed[...], wkv[h], preferred_element_type=jnp.float32
        ).astype(jnp.bfloat16)
        for has, edge, slot, near, via in (
            (has_next, edge_next, 1, f + 1, f - (group - 1)),
            (has_prev, edge_prev, 2, f - 1, f + (group - 1)),
        ):
            if h < NREL:
                @pl.when(edge)
                def _():
                    to_relay(slot, h, {"frame": via}).start()

                @pl.when(has & jnp.logical_not(edge))
                def _():
                    direct(slot, h, {"frame": near}).start()
            else:
                @pl.when(has)
                def _():
                    direct(slot, h, {"frame": near}).start()

        @pl.when(has_up)
        def _():
            direct(3, h, {"row": r + 1}).start()

        @pl.when(has_dn)
        def _():
            direct(4, h, {"row": r - 1}).start()

    q_in.wait()
    for p in range(HEADS // 2):
        both = jnp.dot(
            normed[...], wq[:, 2 * HD * p : 2 * HD * (p + 1)], preferred_element_type=jnp.float32
        ).astype(jnp.bfloat16)
        qs[2 * p] = both[:, :HD]
        qs[2 * p + 1] = both[:, HD:]

    for h in range(NREL):
        for cond, slot, dev in ((relay_next, 1, f + group), (relay_prev, 2, f - group)):
            @pl.when(cond)
            def _():
                to_relay(slot, h, {"frame": f}).wait_recv()
                onward(slot, h, {"frame": dev}).start()

    wo_in.wait()
    for h in range(HEADS):
        for cond, slot in ((has_prev, 1), (has_next, 2), (has_dn, 3), (has_up, 4)):
            @pl.when(cond)
            def _():
                direct(slot, h, {"frame": f}).wait_recv()
        keys = kv[:, h, :, :HD].reshape(KEYS, HD)
        values = kv[:, h, :, HD:].reshape(KEYS, HD)
        scores = lax.dot_general(
            qs[h], keys, (((1,), (1,)), ((), ())), preferred_element_type=jnp.float32
        ) * HD ** (-0.5) + bias[...]
        peak = jnp.max(scores, axis=-1, keepdims=True)
        raised = jnp.exp(scores - peak)
        total = jnp.sum(raised, axis=-1, keepdims=True)
        mix = jnp.dot(raised.astype(jnp.bfloat16), values, preferred_element_type=jnp.float32)
        mixed[:, HD * (h % 2) : HD * (h % 2 + 1)] = (mix / total).astype(jnp.bfloat16)
        if h % 2 == 1:
            part = jnp.dot(
                mixed[...], wo[HD * (h - 1) : HD * (h + 1), :], preferred_element_type=jnp.float32
            )
            if h == 1:
                acc[...] = part
            elif h < HEADS - 1:
                acc[...] += part
            else:
                fin[...] = (
                    x_v[...].astype(jnp.float32) + gate * (acc[...] + part)
                ).astype(jnp.bfloat16)

    hand = copy_to(fin, out_ref, hand_send, hand_recv, {"segment": lax.rem(s + 1, n_seg)})
    hand.start()

    for h in range(HEADS):
        for cond, slot in ((has_next, 1), (has_prev, 2), (has_up, 3), (has_dn, 4)):
            @pl.when(cond)
            def _():
                direct(slot, h, {"frame": f}).wait_send()
    for h in range(NREL):
        @pl.when(relay_next | relay_prev)
        def _():
            onward(1, h, {"frame": f}).wait_send()
    hand.wait()


def body(mesh, clip_tokens, qkv_weight, out_weight, modulation, domain_ids, tile_lists):
    any_space = pl.BlockSpec(memory_space=pl.ANY)
    bf16 = jnp.bfloat16
    dma = pltpu.SemaphoreType.DMA
    out = pl.pallas_call(
        functools.partial(
            kernel, mesh.shape["frame"], mesh.shape["row"], mesh.shape["segment"], 8
        ),
        out_shape=pltpu.VMEM((ROWS, D), bf16),
        in_specs=[pl.BlockSpec(memory_space=pltpu.SMEM)] + [any_space] * 5,
        out_specs=any_space,
        scratch_shapes=[
            pltpu.VMEM((ROWS, D), bf16),
            pltpu.VMEM((ROWS, D), bf16),
            pltpu.VMEM((HEADS, D, 2 * HD), bf16),
            pltpu.VMEM((D, INNER), bf16),
            pltpu.VMEM((INNER, D), bf16),
            pltpu.VMEM((3, modulation.shape[1], D), bf16),
            pltpu.VMEM(tile_lists.shape[2:], jnp.int32),
            pltpu.VMEM((SLOTS, HEADS, ROWS, 2 * HD), bf16),
            pltpu.VMEM((NREL, ROWS, 2 * HD), bf16),
            pltpu.VMEM((HEADS, ROWS, HD), bf16),
            pltpu.VMEM((ROWS, KEYS), jnp.float32),
            pltpu.VMEM((ROWS, 2 * HD), bf16),
            pltpu.VMEM((ROWS, D), jnp.float32),
            pltpu.VMEM((ROWS, D), bf16),
            dma((6,)),
            dma((HEADS, 2)),
            dma((4, HEADS)),
            dma((4, HEADS)),
            dma((NREL,)),
            dma((NREL,)),
            dma,
            dma,
        ],
        compiler_params=pltpu.CompilerParams(
            collective_id=0, has_side_effects=True, vmem_limit_bytes=24 * 2**20
        ),
        name="block",
    )(
        domain_ids,
        *(
            pltpu.with_memory_space_constraint(v, pltpu.HBM)
            for v in (
                clip_tokens.reshape(ROWS, D),
                qkv_weight[0],
                out_weight[0],
                jnp.transpose(modulation[0], (1, 0, 2)),
                tile_lists[0, 0],
            )
        ),
    )
    return out.reshape(clip_tokens.shape)


def solution(mesh):
    return jax.shard_map(
        functools.partial(body, mesh),
        mesh=mesh,
        in_specs=(
            P("segment", "frame", "row", None, None, None),
            P("segment", None, None),
            P("segment", None, None),
            P("segment", None, None, None),
            P("segment"),
            P("frame", "row", None, None),
        ),
        out_specs=P("segment", "frame", "row", None, None, None),
        check_vma=False,
    )
```

```python
import functools

import jax
import jax.numpy as jnp
from jax import lax
from jax.experimental import pallas as pl
from jax.experimental.pallas import tpu as pltpu
from jax.sharding import PartitionSpec as P

MESH = pl.DeviceIdType.MESH
HD = 128
HEADS = 6
INNER = HEADS * HD
D = 1536
ROWS = 128
TILE = 64
SLOTS = 5
KEYS = SLOTS * ROWS
ROUTE = (1, 1, 2, 2, 0, 0)
PARTS = 4
EPS = 1e-06
MASKED = -1e30


def kernel(
    n_frame, n_row, n_seg, group,
    dom_ref, x_hbm, w_hbm, wo_hbm, mod_hbm, lists_hbm,
    out_ref,
    x_v, normed, wkv, wq, wo, mod_v, lists_v,
    kv, relay, qs, bias, mixed, acc, fin,
    in_sem, wkv_sem, send_sem, recv_sem, rsend_sem, rrecv_sem, hand_send, hand_recv,
):
    f = lax.axis_index("frame")
    r = lax.axis_index("row")
    s = lax.axis_index("segment")
    y = lax.rem(f, group)
    g = lax.div(f, group)
    last_g = n_frame // group - 1

    small = [
        pltpu.make_async_copy(x_hbm, x_v, in_sem.at[0]),
        pltpu.make_async_copy(mod_hbm, mod_v, in_sem.at[1]),
        pltpu.make_async_copy(lists_hbm, lists_v, in_sem.at[3]),
    ]
    for c in small:
        c.start()
    kv_in = []
    for h in range(HEADS):
        pair = []
        for part in range(2):
            c = pltpu.make_async_copy(
                w_hbm.at[:, pl.ds(INNER * (1 + part) + HD * h, HD)],
                wkv.at[h, :, pl.ds(HD * part, HD)],
                wkv_sem.at[h, part],
            )
            c.start()
            pair.append(c)
        kv_in.append(pair)
    q_in = pltpu.make_async_copy(w_hbm.at[:, pl.ds(0, INNER)], wq, in_sem.at[4])
    q_in.start()
    wo_in = pltpu.make_async_copy(wo_hbm, wo, in_sem.at[5])
    wo_in.start()

    has_next = f < n_frame - 1
    has_prev = f > 0
    has_up = r < n_row - 1
    has_dn = r > 0
    edge_next = (y == group - 1) & (g < last_g)
    edge_prev = (y == 0) & (g > 0)
    relay_next = (y == 0) & (g < last_g)
    relay_prev = (y == group - 1) & (g > 0)
    back_next = (y == group - 2) & (g < last_g)
    back_prev = (y == 1) & (g > 0)

    barrier = pltpu.get_barrier_semaphore()
    peers = [
        (has_next, {"frame": f + 1}),
        (has_prev, {"frame": f - 1}),
        (has_up, {"row": r + 1}),
        (has_dn, {"row": r - 1}),
        (edge_next, {"frame": f - (group - 1)}),
        (edge_next, {"frame": f + group}),
        (edge_prev, {"frame": f + (group - 1)}),
        (edge_prev, {"frame": f - group}),
        (relay_next, {"frame": f + (group - 1)}),
        (relay_next, {"frame": f + group}),
        (relay_prev, {"frame": f - (group - 1)}),
        (relay_prev, {"frame": f - group}),
        (edge_next, {"frame": f + 2}),
        (edge_prev, {"frame": f - 2}),
        (back_next, {"frame": f + 2}),
        (back_prev, {"frame": f - 2}),
        (None, {"segment": lax.rem(s + n_seg - 1, n_seg)}),
    ]
    def when(cond):
        return (lambda act: act()) if cond is None else pl.when(cond)

    for cond, dev in peers:
        @when(cond)
        def _(dev=dev):
            pl.semaphore_signal(barrier, inc=1, device_id=dev, device_id_type=MESH)

    for cond, slot in ((f == 0, 1), (f == n_frame - 1, 2), (r == 0, 3), (r == n_row - 1, 4)):
        @pl.when(cond)
        def _(slot=slot):
            kv[slot] = jnp.zeros((HEADS, ROWS, 2 * HD), jnp.bfloat16)

    for c in small:
        c.wait()

    domains = mod_v.shape[1]
    mine = lax.broadcasted_iota(jnp.int32, (domains, D), 0) == dom_ref[0]

    def of_domain(i):
        return jnp.sum(jnp.where(mine, mod_v[i].astype(jnp.float32), 0.0), axis=0, keepdims=True)

    shift = of_domain(0)
    scale = 1.0 + of_domain(1)
    gate = of_domain(2)

    def norm_rows(i, _):
        rows = pl.ds(pl.multiple_of(i * 16, 16), 16)
        values = x_v[rows, :].astype(jnp.float32)
        mean = jnp.sum(values, axis=-1, keepdims=True) * (1.0 / D)
        centered = values - mean
        var = jnp.sum(centered * centered, axis=-1, keepdims=True) * (1.0 / D)
        normed[rows, :] = (centered * lax.rsqrt(var + EPS) * scale + shift).astype(jnp.bfloat16)
        return 0

    lax.fori_loop(0, ROWS // 16, norm_rows, 0, unroll=2)

    lists = lists_v[...]
    cand = lax.broadcasted_iota(jnp.int32, (2, KEYS), 1) // TILE
    hit = jnp.zeros((2, KEYS), jnp.float32)
    for j in range(lists.shape[1]):
        hit = jnp.where(cand == lists[:, j : j + 1], 1.0, hit)
    open_keys = jnp.where(hit > 0.5, 0.0, MASKED)
    for t in range(2):
        bias[pl.ds(t * TILE, TILE), :] = jnp.broadcast_to(open_keys[t : t + 1], (TILE, KEYS))

    greeted = 1
    for cond, _ in peers[:-1]:
        greeted += cond.astype(jnp.int32)
    pl.semaphore_wait(barrier, greeted)

    def copy_to(src, dst, send, recv, dev):
        return pltpu.make_async_remote_copy(
            src_ref=src, dst_ref=dst, send_sem=send, recv_sem=recv,
            device_id=dev, device_id_type=MESH,
        )

    def direct(slot, h, dev):
        return copy_to(kv.at[0, h], kv.at[slot, h], send_sem.at[slot - 1, h], recv_sem.at[slot - 1, h], dev)

    def to_relay(slot, h, dev):
        return copy_to(kv.at[0, h], relay.at[h], send_sem.at[slot - 1, h], rrecv_sem.at[h], dev)

    def onward(slot, h, dev):
        return copy_to(relay.at[h], kv.at[slot, h], rsend_sem.at[h], recv_sem.at[slot - 1, h], dev)

    def back(slot, h, dev):
        return copy_to(kv.at[3 - slot, h], kv.at[slot, h], rsend_sem.at[h], recv_sem.at[slot - 1, h], dev)

    for h in range(HEADS):
        for c in kv_in[h]:
            c.wait()
        kv[0, h] = jnp.dot(
            normed[...], wkv[h], preferred_element_type=jnp.float32
        ).astype(jnp.bfloat16)
        for has, edge, slot, near, via in (
            (has_next, edge_next, 1, f + 1, f - (group - 1)),
            (has_prev, edge_prev, 2, f - 1, f + (group - 1)),
        ):
            if ROUTE[h] == 1:
                @pl.when(edge)
                def _():
                    to_relay(slot, h, {"frame": via}).start()

            @pl.when(has & jnp.logical_not(edge) if ROUTE[h] else has)
            def _():
                direct(slot, h, {"frame": near}).start()

        @pl.when(has_up)
        def _():
            direct(3, h, {"row": r + 1}).start()

        @pl.when(has_dn)
        def _():
            direct(4, h, {"row": r - 1}).start()

    q_in.wait()
    for p in range(HEADS // 2):
        both = jnp.dot(
            normed[...], wq[:, 2 * HD * p : 2 * HD * (p + 1)], preferred_element_type=jnp.float32
        ).astype(jnp.bfloat16)
        qs[2 * p] = both[:, :HD]
        qs[2 * p + 1] = both[:, HD:]

    for h in range(HEADS):
        if ROUTE[h] == 1:
            for cond, slot, dev in ((relay_next, 1, f + group), (relay_prev, 2, f - group)):
                @pl.when(cond)
                def _():
                    to_relay(slot, h, {"frame": f}).wait_recv()
                    onward(slot, h, {"frame": dev}).start()
        elif ROUTE[h] == 2:
            for cond, slot, dev in ((back_next, 1, f + 2), (back_prev, 2, f - 2)):
                @pl.when(cond)
                def _():
                    direct(3 - slot, h, {"frame": f}).wait_recv()
                    back(slot, h, {"frame": dev}).start()

    wo_in.wait()
    for h in range(HEADS):
        for cond, slot, taken in (
            (has_prev, 1, back_prev),
            (has_next, 2, back_next),
            (has_dn, 3, None),
            (has_up, 4, None),
        ):
            if ROUTE[h] == 2 and taken is not None:
                cond = cond & jnp.logical_not(taken)

            @pl.when(cond)
            def _():
                direct(slot, h, {"frame": f}).wait_recv()

        keys = kv[:, h, :, :HD].reshape(KEYS, HD)
        values = kv[:, h, :, HD:].reshape(KEYS, HD)
        scores = lax.dot_general(
            qs[h], keys, (((1,), (1,)), ((), ())), preferred_element_type=jnp.float32
        ) * HD ** (-0.5) + bias[...]
        peak = jnp.max(scores, axis=-1, keepdims=True)
        raised = jnp.exp(scores - peak)
        total = jnp.sum(raised, axis=-1, keepdims=True)
        mix = jnp.dot(raised.astype(jnp.bfloat16), values, preferred_element_type=jnp.float32)
        mixed[:, HD * (h % 2) : HD * (h % 2 + 1)] = (mix / total).astype(jnp.bfloat16)
        if h % 2 == 1 and h < HEADS - 1:
            part = jnp.dot(
                mixed[...], wo[HD * (h - 1) : HD * (h + 1), :], preferred_element_type=jnp.float32
            )
            acc[...] = part if h == 1 else acc[...] + part

    hands = []
    for p in range(PARTS):
        cols = pl.ds(D // PARTS * p, D // PARTS)
        part = jnp.dot(mixed[...], wo[INNER - 2 * HD :, cols], preferred_element_type=jnp.float32)
        fin[:, cols] = (
            x_v[:, cols].astype(jnp.float32)
            + gate[:, D // PARTS * p : D // PARTS * (p + 1)] * (acc[:, cols] + part)
        ).astype(jnp.bfloat16)
        c = copy_to(
            fin.at[:, cols], out_ref.at[:, cols], hand_send.at[p], hand_recv.at[p],
            {"segment": lax.rem(s + 1, n_seg)},
        )
        c.start()
        hands.append(c)

    for h in range(HEADS):
        for has, edge, slot in ((has_next, edge_next, 1), (has_prev, edge_prev, 2), (has_up, None, 3), (has_dn, None, 4)):
            if ROUTE[h] == 2 and edge is not None:
                has = has & jnp.logical_not(edge)

            @pl.when(has)
            def _():
                direct(slot, h, {"frame": f}).wait_send()
        if ROUTE[h]:
            @pl.when((relay_next | relay_prev) if ROUTE[h] == 1 else (back_next | back_prev))
            def _():
                onward(1, h, {"frame": f}).wait_send()
    for c in hands:
        c.wait()


def body(mesh, clip_tokens, qkv_weight, out_weight, modulation, domain_ids, tile_lists):
    any_space = pl.BlockSpec(memory_space=pl.ANY)
    bf16 = jnp.bfloat16
    dma = pltpu.SemaphoreType.DMA
    out = pl.pallas_call(
        functools.partial(
            kernel, mesh.shape["frame"], mesh.shape["row"], mesh.shape["segment"], 8
        ),
        out_shape=pltpu.VMEM((ROWS, D), bf16),
        in_specs=[pl.BlockSpec(memory_space=pltpu.SMEM)] + [any_space] * 5,
        out_specs=any_space,
        scratch_shapes=[
            pltpu.VMEM((ROWS, D), bf16),
            pltpu.VMEM((ROWS, D), bf16),
            pltpu.VMEM((HEADS, D, 2 * HD), bf16),
            pltpu.VMEM((D, INNER), bf16),
            pltpu.VMEM((INNER, D), bf16),
            pltpu.VMEM((3, modulation.shape[1], D), bf16),
            pltpu.VMEM(tile_lists.shape[2:], jnp.int32),
            pltpu.VMEM((SLOTS, HEADS, ROWS, 2 * HD), bf16),
            pltpu.VMEM((HEADS, ROWS, 2 * HD), bf16),
            pltpu.VMEM((HEADS, ROWS, HD), bf16),
            pltpu.VMEM((ROWS, KEYS), jnp.float32),
            pltpu.VMEM((ROWS, 2 * HD), bf16),
            pltpu.VMEM((ROWS, D), jnp.float32),
            pltpu.VMEM((ROWS, D), bf16),
            dma((6,)),
            dma((HEADS, 2)),
            dma((4, HEADS)),
            dma((4, HEADS)),
            dma((HEADS,)),
            dma((HEADS,)),
            dma((PARTS,)),
            dma((PARTS,)),
        ],
        compiler_params=pltpu.CompilerParams(
            collective_id=0, has_side_effects=True, vmem_limit_bytes=24 * 2**20
        ),
        name="block",
    )(
        domain_ids,
        *(
            pltpu.with_memory_space_constraint(v, pltpu.HBM)
            for v in (
                clip_tokens.reshape(ROWS, D),
                qkv_weight[0],
                out_weight[0],
                jnp.transpose(modulation[0], (1, 0, 2)),
                tile_lists[0, 0],
            )
        ),
    )
    return out.reshape(clip_tokens.shape)


def solution(mesh):
    return jax.shard_map(
        functools.partial(body, mesh),
        mesh=mesh,
        in_specs=(
            P("segment", "frame", "row", None, None, None),
            P("segment", None, None),
            P("segment", None, None),
            P("segment", None, None, None),
            P("segment"),
            P("frame", "row", None, None),
        ),
        out_specs=P("segment", "frame", "row", None, None, None),
        check_vma=False,
    )
```

```python
import functools

import jax
import jax.numpy as jnp
from jax import lax
from jax.experimental import pallas as pl
from jax.experimental.pallas import tpu as pltpu
from jax.sharding import PartitionSpec as P

MESH = pl.DeviceIdType.MESH
HD = 128
HEADS = 6
INNER = HEADS * HD
D = 1536
ROWS = 128
TILE = 64
SLOTS = 5
KEYS = SLOTS * ROWS
ROUTE = (1, 1, 2, 2, 0, 0)
PARTS = 4
EPS = 1e-06
MASKED = -1e30


def kernel(
    n_frame, n_row, n_seg, group,
    dom_ref, x_hbm, w_hbm, wo_hbm, mod_hbm, lists_hbm,
    out_ref,
    x_v, normed, wkv, wq, wo, mod_v, lists_v,
    kv, relay, qs, bias, mixed, acc, fin,
    in_sem, wkv_sem, send_sem, recv_sem, rsend_sem, rrecv_sem, hand_send, hand_recv,
):
    f = lax.axis_index("frame")
    r = lax.axis_index("row")
    s = lax.axis_index("segment")
    y = lax.rem(f, group)
    g = lax.div(f, group)
    last_g = n_frame // group - 1

    small = [
        pltpu.make_async_copy(x_hbm, x_v, in_sem.at[0]),
        pltpu.make_async_copy(mod_hbm, mod_v, in_sem.at[1]),
        pltpu.make_async_copy(lists_hbm, lists_v, in_sem.at[3]),
    ]
    for c in small:
        c.start()
    has_next = f < n_frame - 1
    has_prev = f > 0
    has_up = r < n_row - 1
    has_dn = r > 0
    edge_next = (y == group - 1) & (g < last_g)
    edge_prev = (y == 0) & (g > 0)
    relay_next = (y == 0) & (g < last_g)
    relay_prev = (y == group - 1) & (g > 0)
    back_next = (y == group - 2) & (g < last_g)
    back_prev = (y == 1) & (g > 0)

    barrier = pltpu.get_barrier_semaphore()
    peers = [
        (has_next, {"frame": f + 1}),
        (has_prev, {"frame": f - 1}),
        (has_up, {"row": r + 1}),
        (has_dn, {"row": r - 1}),
        (edge_next, {"frame": f - (group - 1)}),
        (edge_next, {"frame": f + group}),
        (edge_prev, {"frame": f + (group - 1)}),
        (edge_prev, {"frame": f - group}),
        (relay_next, {"frame": f + (group - 1)}),
        (relay_next, {"frame": f + group}),
        (relay_prev, {"frame": f - (group - 1)}),
        (relay_prev, {"frame": f - group}),
        (edge_next, {"frame": f + 2}),
        (edge_prev, {"frame": f - 2}),
        (back_next, {"frame": f + 2}),
        (back_prev, {"frame": f - 2}),
        (None, {"segment": lax.rem(s + n_seg - 1, n_seg)}),
    ]
    def when(cond):
        return (lambda act: act()) if cond is None else pl.when(cond)

    for cond, dev in peers:
        @when(cond)
        def _(dev=dev):
            pl.semaphore_signal(barrier, inc=1, device_id=dev, device_id_type=MESH)

    kv_in = []
    for h in range(HEADS):
        pair = []
        for part in range(2):
            c = pltpu.make_async_copy(
                w_hbm.at[:, pl.ds(INNER * (1 + part) + HD * h, HD)],
                wkv.at[h, :, pl.ds(HD * part, HD)],
                wkv_sem.at[h, part],
            )
            c.start()
            pair.append(c)
        kv_in.append(pair)
    q_in = pltpu.make_async_copy(w_hbm.at[:, pl.ds(0, INNER)], wq, in_sem.at[4])
    q_in.start()
    wo_in = pltpu.make_async_copy(wo_hbm, wo, in_sem.at[5])
    wo_in.start()

    for cond, slot in ((f == 0, 1), (f == n_frame - 1, 2), (r == 0, 3), (r == n_row - 1, 4)):
        @pl.when(cond)
        def _(slot=slot):
            kv[slot] = jnp.zeros((HEADS, ROWS, 2 * HD), jnp.bfloat16)

    for c in small:
        c.wait()

    domains = mod_v.shape[1]
    mine = lax.broadcasted_iota(jnp.int32, (domains, D), 0) == dom_ref[0]

    def of_domain(i):
        return jnp.sum(jnp.where(mine, mod_v[i].astype(jnp.float32), 0.0), axis=0, keepdims=True)

    shift = of_domain(0)
    scale = 1.0 + of_domain(1)
    gate = of_domain(2)

    def norm_rows(i, _):
        rows = pl.ds(pl.multiple_of(i * 16, 16), 16)
        values = x_v[rows, :].astype(jnp.float32)
        mean = jnp.sum(values, axis=-1, keepdims=True) * (1.0 / D)
        centered = values - mean
        var = jnp.sum(centered * centered, axis=-1, keepdims=True) * (1.0 / D)
        normed[rows, :] = (centered * lax.rsqrt(var + EPS) * scale + shift).astype(jnp.bfloat16)
        return 0

    lax.fori_loop(0, ROWS // 16, norm_rows, 0, unroll=2)

    lists = lists_v[...]
    cand = lax.broadcasted_iota(jnp.int32, (2, KEYS), 1) // TILE
    hit = jnp.zeros((2, KEYS), jnp.float32)
    for j in range(lists.shape[1]):
        hit = jnp.where(cand == lists[:, j : j + 1], 1.0, hit)
    open_keys = jnp.where(hit > 0.5, 0.0, MASKED)
    for t in range(2):
        bias[pl.ds(t * TILE, TILE), :] = jnp.broadcast_to(open_keys[t : t + 1], (TILE, KEYS))

    greeted = 1
    for cond, _ in peers[:-1]:
        greeted += cond.astype(jnp.int32)
    pl.semaphore_wait(barrier, greeted)

    def copy_to(src, dst, send, recv, dev):
        return pltpu.make_async_remote_copy(
            src_ref=src, dst_ref=dst, send_sem=send, recv_sem=recv,
            device_id=dev, device_id_type=MESH,
        )

    def direct(slot, h, dev):
        return copy_to(kv.at[0, h], kv.at[slot, h], send_sem.at[slot - 1, h], recv_sem.at[slot - 1, h], dev)

    def to_relay(slot, h, dev):
        return copy_to(kv.at[0, h], relay.at[h], send_sem.at[slot - 1, h], rrecv_sem.at[h], dev)

    def onward(slot, h, dev):
        return copy_to(relay.at[h], kv.at[slot, h], rsend_sem.at[h], recv_sem.at[slot - 1, h], dev)

    def back(slot, h, dev):
        return copy_to(kv.at[3 - slot, h], kv.at[slot, h], rsend_sem.at[h], recv_sem.at[slot - 1, h], dev)

    for h in range(HEADS):
        for c in kv_in[h]:
            c.wait()
        kv[0, h] = jnp.dot(
            normed[...], wkv[h], preferred_element_type=jnp.float32
        ).astype(jnp.bfloat16)
        for has, edge, slot, near, via in (
            (has_next, edge_next, 1, f + 1, f - (group - 1)),
            (has_prev, edge_prev, 2, f - 1, f + (group - 1)),
        ):
            if ROUTE[h] == 1:
                @pl.when(edge)
                def _():
                    to_relay(slot, h, {"frame": via}).start()

            @pl.when(has & jnp.logical_not(edge) if ROUTE[h] else has)
            def _():
                direct(slot, h, {"frame": near}).start()

        @pl.when(has_up)
        def _():
            direct(3, h, {"row": r + 1}).start()

        @pl.when(has_dn)
        def _():
            direct(4, h, {"row": r - 1}).start()

    q_in.wait()
    for p in range(HEADS // 2):
        both = jnp.dot(
            normed[...], wq[:, 2 * HD * p : 2 * HD * (p + 1)], preferred_element_type=jnp.float32
        ).astype(jnp.bfloat16)
        qs[2 * p] = both[:, :HD]
        qs[2 * p + 1] = both[:, HD:]

    for h in range(HEADS):
        if ROUTE[h] == 1:
            for cond, slot, dev in ((relay_next, 1, f + group), (relay_prev, 2, f - group)):
                @pl.when(cond)
                def _():
                    to_relay(slot, h, {"frame": f}).wait_recv()
                    onward(slot, h, {"frame": dev}).start()
        elif ROUTE[h] == 2:
            for cond, slot, dev in ((back_next, 1, f + 2), (back_prev, 2, f - 2)):
                @pl.when(cond)
                def _():
                    direct(3 - slot, h, {"frame": f}).wait_recv()
                    back(slot, h, {"frame": dev}).start()

    wo_in.wait()
    for h in range(HEADS):
        for cond, slot, taken in (
            (has_prev, 1, back_prev),
            (has_next, 2, back_next),
            (has_dn, 3, None),
            (has_up, 4, None),
        ):
            if ROUTE[h] == 2 and taken is not None:
                cond = cond & jnp.logical_not(taken)

            @pl.when(cond)
            def _():
                direct(slot, h, {"frame": f}).wait_recv()

        keys = kv[:, h, :, :HD].reshape(KEYS, HD)
        values = kv[:, h, :, HD:].reshape(KEYS, HD)
        scores = lax.dot_general(
            qs[h], keys, (((1,), (1,)), ((), ())), preferred_element_type=jnp.float32
        ) * HD ** (-0.5) + bias[...]
        peak = jnp.max(scores, axis=-1, keepdims=True)
        raised = jnp.exp(scores - peak)
        total = jnp.sum(raised, axis=-1, keepdims=True)
        mix = jnp.dot(raised.astype(jnp.bfloat16), values, preferred_element_type=jnp.float32)
        mixed[:, HD * (h % 2) : HD * (h % 2 + 1)] = (mix / total).astype(jnp.bfloat16)
        if h % 2 == 1 and h < HEADS - 1:
            part = jnp.dot(
                mixed[...], wo[HD * (h - 1) : HD * (h + 1), :], preferred_element_type=jnp.float32
            )
            acc[...] = part if h == 1 else acc[...] + part

    hands = []
    for p in range(PARTS):
        cols = pl.ds(D // PARTS * p, D // PARTS)
        part = jnp.dot(mixed[...], wo[INNER - 2 * HD :, cols], preferred_element_type=jnp.float32)
        fin[:, cols] = (
            x_v[:, cols].astype(jnp.float32)
            + gate[:, D // PARTS * p : D // PARTS * (p + 1)] * (acc[:, cols] + part)
        ).astype(jnp.bfloat16)
        c = copy_to(
            fin.at[:, cols], out_ref.at[:, cols], hand_send.at[p], hand_recv.at[p],
            {"segment": lax.rem(s + 1, n_seg)},
        )
        c.start()
        hands.append(c)

    for h in range(HEADS):
        for has, edge, slot in ((has_next, edge_next, 1), (has_prev, edge_prev, 2), (has_up, None, 3), (has_dn, None, 4)):
            if ROUTE[h] == 2 and edge is not None:
                has = has & jnp.logical_not(edge)

            @pl.when(has)
            def _():
                direct(slot, h, {"frame": f}).wait_send()
        if ROUTE[h]:
            @pl.when((relay_next | relay_prev) if ROUTE[h] == 1 else (back_next | back_prev))
            def _():
                onward(1, h, {"frame": f}).wait_send()
    for c in hands:
        c.wait()


def body(mesh, clip_tokens, qkv_weight, out_weight, modulation, domain_ids, tile_lists):
    any_space = pl.BlockSpec(memory_space=pl.ANY)
    bf16 = jnp.bfloat16
    dma = pltpu.SemaphoreType.DMA
    out = pl.pallas_call(
        functools.partial(
            kernel, mesh.shape["frame"], mesh.shape["row"], mesh.shape["segment"], 8
        ),
        out_shape=pltpu.VMEM((ROWS, D), bf16),
        in_specs=[pl.BlockSpec(memory_space=pltpu.SMEM)] + [any_space] * 5,
        out_specs=any_space,
        scratch_shapes=[
            pltpu.VMEM((ROWS, D), bf16),
            pltpu.VMEM((ROWS, D), bf16),
            pltpu.VMEM((HEADS, D, 2 * HD), bf16),
            pltpu.VMEM((D, INNER), bf16),
            pltpu.VMEM((INNER, D), bf16),
            pltpu.VMEM((3, modulation.shape[1], D), bf16),
            pltpu.VMEM(tile_lists.shape[2:], jnp.int32),
            pltpu.VMEM((SLOTS, HEADS, ROWS, 2 * HD), bf16),
            pltpu.VMEM((HEADS, ROWS, 2 * HD), bf16),
            pltpu.VMEM((HEADS, ROWS, HD), bf16),
            pltpu.VMEM((ROWS, KEYS), jnp.float32),
            pltpu.VMEM((ROWS, 2 * HD), bf16),
            pltpu.VMEM((ROWS, D), jnp.float32),
            pltpu.VMEM((ROWS, D), bf16),
            dma((6,)),
            dma((HEADS, 2)),
            dma((4, HEADS)),
            dma((4, HEADS)),
            dma((HEADS,)),
            dma((HEADS,)),
            dma((PARTS,)),
            dma((PARTS,)),
        ],
        compiler_params=pltpu.CompilerParams(
            collective_id=0, has_side_effects=True, vmem_limit_bytes=24 * 2**20
        ),
        name="block",
    )(
        domain_ids,
        *(
            pltpu.with_memory_space_constraint(v, pltpu.HBM)
            for v in (
                clip_tokens.reshape(ROWS, D),
                qkv_weight[0],
                out_weight[0],
                jnp.transpose(modulation[0], (1, 0, 2)),
                tile_lists[0, 0],
            )
        ),
    )
    return out.reshape(clip_tokens.shape)


def solution(mesh):
    return jax.shard_map(
        functools.partial(body, mesh),
        mesh=mesh,
        in_specs=(
            P("segment", "frame", "row", None, None, None),
            P("segment", None, None),
            P("segment", None, None),
            P("segment", None, None, None),
            P("segment"),
            P("frame", "row", None, None),
        ),
        out_specs=P("segment", "frame", "row", None, None, None),
        check_vma=False,
    )
```
